256 devices in a mesh: ctx: 32 (over y, x, core), head: 8 (over z).
Axes of the slice: x: 4, y: 4, z: 8, core: 2. Of those that a mesh axis runs over, the one named last changes fastest.
Arguments:
- queries: bfloat16 [16384, 4096], P('ctx', 'head'), may hold values from -0.59765625 to 0.59765625
- keys: bfloat16 [16384, 4096], P('ctx', 'head'), may hold values from -0.59765625 to 0.59765625
- values: bfloat16 [16384, 4096], P('ctx', 'head'), may hold values from -6 to 6
- gates: float32 [32, 9, 16384], P('head', None, 'ctx'), may hold values from 0.05 to 1
- segment_ids: int32 [16384], P('ctx'), may hold values from 0 to 2, never falling along the last dimension, each value on 1 to 12288 neighbouring positions
- out_weight: bfloat16 [4096, 4096], P('head'), may hold values from -0.09375 to 0.09375
- out_grad: bfloat16 [16384, 4096], P('ctx', 'head'), may hold values from -0.59765625 to 0.59765625
Outputs:
- mixed: bfloat16 [16384, 4096], P('ctx', 'head')
- grad_queries: bfloat16 [16384, 4096], P('ctx', 'head')
- grad_keys: bfloat16 [16384, 4096], P('ctx', 'head')
- grad_values: bfloat16 [16384, 4096], P('ctx', 'head')
The draws below stay inside these ranges and needn't reach their ends.
Inputs may be any that keep to these rules, and one draw needn't show every extreme that they name: `segment_ids`: segment ids never fall along the sequence: each document is one run of consecutive tokens; one document has exactly 12288 tokens.
All inputs are finite; a program needn't handle non-finite values.
Results may differ from the reference program's by a relative error of at most 0.018.
Values may be sent and summed in bfloat16 or wider, within the bound.
No kernel may reach another device: no remote copies, remote signals or barrier semaphores. Data moves between devices by JAX's collectives and lax.ppermute only.
A program may use at most 64 MiB of HBM per device.

```python
import math
import jax
import jax.numpy as jnp
import numpy as np
from jax import lax

D = 4096
HEADS = 32
DK = 128
DV = 128
SPAN = 64
DOCS = 3
TOK_DEV = 512
TOKENS = 16384
NEAR_LEVELS = 4
LEVELS = 9
N_CTX = 32
N_HEAD = 8


def shard_levels(stream_key, extent, shards, least, top_value):
    factor_of, own = 1.0, jax.random.fold_in(stream_key, 6)
    for axis_at, parts in shards:
        steps = jnp.exp(jax.random.uniform(jax.random.fold_in(own, axis_at), (parts,), jnp.float32, least / len(shards), top_value / len(shards)))
        factor_of = factor_of * jnp.repeat(steps, extent[axis_at] // parts).reshape([-1 if axis == axis_at else 1 for axis in range(len(extent))])
    return factor_of


def profile(number_of, total, reach, skew):
    weights = [(1 << 20) // math.isqrt(rank ** skew) + 1 for rank in range(2, number_of + 1)]
    spare, holding = total - reach - (number_of - 1), [1] * (number_of - 1)
    while spare > 0:
        movable = [i for i in range(number_of - 1) if holding[i] < reach]
        pool, left = sum([weights[i] for i in movable]), spare
        for i in movable:
            more = min(reach - holding[i], max(1, left * weights[i] // pool), spare)
            holding[i] = holding[i] + more
            spare = spare - more
    return np.array([reach] + holding)


def ragged(key, amount, total, limit, lean):
    if amount == 2:
        one = jax.random.randint(key, (), max(1, total - limit), min(limit, total - 1) + 1)
        return jnp.stack([one, total - one])
    sizes = jnp.asarray(profile(amount, total, limit, lean), jnp.int32)
    couples = (amount - 1) // 2
    giver, taker = sizes[1:1 + 2 * couples:2], sizes[2:2 + 2 * couples:2]
    room = jnp.minimum(giver - 1, limit - taker)
    passed = jax.random.randint(jax.random.fold_in(key, 1), (couples,), 0, 1 << 20) % (room + 1)
    sizes = sizes.at[1:1 + 2 * couples:2].set(giver - passed).at[2:2 + 2 * couples:2].set(taker + passed)
    return sizes[jax.random.permutation(jax.random.fold_in(key, 2), amount)]


def scatter_about(own_key, dims, scale, limit, pieces=(), held_as=jnp.bfloat16):
    level = shard_levels(own_key, dims, pieces, -0.22, 0.18) if pieces else 1.0
    values = jax.random.normal(own_key, dims, jnp.float32) * scale * level
    return jnp.minimum(jnp.maximum(values, -limit), limit).astype(held_as)


def setup_inputs(seed: int = 0) -> dict:
    arg_keys = jax.random.split(jax.random.key(seed), 8)
    queries = scatter_about(arg_keys[0], (TOKENS, HEADS * DK), 0.1, 0.59765625, ((0, 32), (1, 8)))
    keys = scatter_about(arg_keys[1], (TOKENS, HEADS * DK), 0.1, 0.59765625, ((0, 32), (1, 8)))
    values = scatter_about(arg_keys[2], (TOKENS, HEADS * DV), 1.0, 6.0, ((0, 32), (1, 8)))
    gates = jnp.clip(jnp.exp(math.log(1.0) - 2.9957323 * jax.random.uniform(arg_keys[3], (HEADS, LEVELS, TOKENS), jnp.float32) ** shard_levels(arg_keys[3], (HEADS, LEVELS, TOKENS), ((0, 8), (2, 32)), -0.2, 0.2)), 0.05, 1.0)
    segment_ids = jnp.searchsorted(jnp.cumsum(ragged(arg_keys[4], DOCS, TOKENS, TOKENS * 3 // 4, 0)), jnp.arange(TOKENS), side="right").astype(jnp.int32)
    out_weight = scatter_about(arg_keys[5], (HEADS * DV, D), (HEADS * DV) ** -0.5, 0.09375, ((0, 8),))
    out_grad = scatter_about(arg_keys[6], (TOKENS, D), 0.1, 0.59765625, ((0, 32), (1, 8)))
    return {"queries": queries, "keys": keys, "values": values, "gates": gates, "segment_ids": segment_ids, "out_weight": out_weight, "out_grad": out_grad}


highest = lax.Precision.HIGHEST


def level_table(count):
    span_ids = jnp.arange(count, dtype=jnp.int32) // SPAN
    differ = jnp.bitwise_xor(span_ids[:, None], span_ids[None, :])
    levels = jnp.zeros((count, count), jnp.int32)
    for section in range(NEAR_LEVELS - 1):
        levels = levels + (differ >= (1 << section)).astype(jnp.int32)
    return levels


def near_block(block, levels):
    query, key, value, grad_out, gate, segment = block
    count = query.shape[0]
    positions = jnp.arange(count, dtype=jnp.int32)
    allowed = (positions[:, None] >= positions[None, :]) & (segment[:, None] == segment[None, :])
    weight = jnp.zeros((count, count), jnp.float32)
    for level_id in range(NEAR_LEVELS):
        weight = weight + jnp.where(levels == level_id, gate[level_id][:, None], jnp.float32(0))
    weight = jnp.where(allowed, weight, jnp.float32(0))
    scores = jnp.dot(query, key.T, preferred_element_type=jnp.float32)
    near_probs = (weight * scores).astype(jnp.bfloat16)
    result = jnp.dot(near_probs, value, preferred_element_type=jnp.float32)
    value_scores = jnp.dot(grad_out, value.T, preferred_element_type=jnp.float32)
    grad_scores = (weight * value_scores).astype(jnp.bfloat16)
    grad_query = jnp.dot(grad_scores, key, preferred_element_type=jnp.float32)
    grad_key = jnp.dot(grad_scores.T, query, preferred_element_type=jnp.float32)
    grad_value = jnp.dot(near_probs.T, grad_out, preferred_element_type=jnp.float32)
    return result, grad_query, grad_key, grad_value


def reference(queries, keys, values, gates, segment_ids, out_weight, out_grad):
    grad_attention = jnp.dot(out_grad, out_weight.T, preferred_element_type=jnp.float32).astype(jnp.bfloat16)
    levels = level_table(TOK_DEV)

    def split_heads(array, width):
        return array.reshape(TOKENS, HEADS, width).transpose(1, 0, 2)

    def near_one(block):
        return near_block(block, levels)

    def head_terms(items):
        query, key, value, grad_out, gate = items
        blocks = (query.reshape(N_CTX, TOK_DEV, DK), key.reshape(N_CTX, TOK_DEV, DK),
                  value.reshape(N_CTX, TOK_DEV, DV), grad_out.reshape(N_CTX, TOK_DEV, DV),
                  gate.reshape(LEVELS, N_CTX, TOK_DEV).transpose(1, 0, 2),
                  segment_ids.reshape(N_CTX, TOK_DEV))
        near = jax.vmap(near_one)(blocks)
        result = near[0].reshape(TOKENS, DV)
        grad_query = near[1].reshape(TOKENS, DK)
        grad_key = near[2].reshape(TOKENS, DK)
        grad_value = near[3].reshape(TOKENS, DV)
        query_wide = query.astype(jnp.float32)
        key_wide = key.astype(jnp.float32)
        value_wide = value.astype(jnp.float32)
        grad_wide = grad_out.astype(jnp.float32)
        for level_id in range(NEAR_LEVELS, LEVELS):
            run = SPAN * 2 ** (level_id - 1)
            groups = TOKENS // (2 * run)
            query_runs = query_wide.reshape(groups, 2, run, DK)
            key_runs = key_wide.reshape(groups, 2, run, DK)
            value_runs = value_wide.reshape(groups, 2, run, DV)
            grad_runs = grad_wide.reshape(groups, 2, run, DV)
            segment_runs = segment_ids.reshape(groups, 2, run)
            end_seg = segment_runs[:, 0, run - 1]
            low_keep = (segment_runs[:, 0, :] == end_seg[:, None]).astype(jnp.float32)
            high_keep = (segment_runs[:, 1, :] == end_seg[:, None]).astype(jnp.float32)
            high_gate = gate[level_id].reshape(groups, 2, run)[:, 1, :] * high_keep
            state = jnp.einsum("gsd,gse->gde", key_runs[:, 0] * low_keep[..., None], value_runs[:, 0], precision=highest)
            dual = jnp.einsum("gtd,gte->gde", query_runs[:, 1] * high_gate[..., None], grad_runs[:, 1], precision=highest)
            high_out = jnp.einsum("gtd,gde->gte", query_runs[:, 1], state, precision=highest) * high_gate[..., None]
            high_dq = jnp.einsum("gte,gde->gtd", grad_runs[:, 1], state, precision=highest) * high_gate[..., None]
            low_dk = jnp.einsum("gse,gde->gsd", value_runs[:, 0], dual, precision=highest) * low_keep[..., None]
            low_dv = jnp.einsum("gsd,gde->gse", key_runs[:, 0], dual, precision=highest) * low_keep[..., None]
            result = result + jnp.stack([jnp.zeros_like(high_out), high_out], 1).reshape(TOKENS, DV)
            grad_query = grad_query + jnp.stack([jnp.zeros_like(high_dq), high_dq], 1).reshape(TOKENS, DK)
            grad_key = grad_key + jnp.stack([low_dk, jnp.zeros_like(low_dk)], 1).reshape(TOKENS, DK)
            grad_value = grad_value + jnp.stack([low_dv, jnp.zeros_like(low_dv)], 1).reshape(TOKENS, DV)
        return result, grad_query, grad_key, grad_value

    terms = lax.map(head_terms, (split_heads(queries, DK), split_heads(keys, DK), split_heads(values, DV),
                                 split_heads(grad_attention, DV), gates))
    attention = terms[0].transpose(1, 0, 2).reshape(TOKENS, HEADS * DV).astype(jnp.bfloat16)
    group = HEADS * DV // N_HEAD
    mixed = jnp.zeros((TOKENS, D), jnp.float32)
    for part_id in range(N_HEAD):
        term = jnp.dot(attention[:, part_id * group:(part_id + 1) * group],
                       out_weight[part_id * group:(part_id + 1) * group], preferred_element_type=jnp.float32)
        rounded = lax.optimization_barrier(term.astype(jnp.bfloat16))
        mixed = mixed + rounded.astype(jnp.float32)
    grad_queries = terms[1].transpose(1, 0, 2).reshape(TOKENS, HEADS * DK).astype(jnp.bfloat16)
    grad_keys = terms[2].transpose(1, 0, 2).reshape(TOKENS, HEADS * DK).astype(jnp.bfloat16)
    grad_values = terms[3].transpose(1, 0, 2).reshape(TOKENS, HEADS * DV).astype(jnp.bfloat16)
    return (mixed.astype(jnp.bfloat16), grad_queries, grad_keys, grad_values)
```

```python
import functools

import jax
import jax.numpy as jnp
from jax import lax
from jax.experimental import pallas as pl
from jax.experimental.pallas import tpu as pltpu
from jax.sharding import PartitionSpec as P

SPAN = 64
NEAR = 4
FAR = 5
ROWS = 512
HALF = 256
HEADS = 4
WIDTH = 128
MARKS = 16
STATE = HEADS * WIDTH
F32 = jnp.float32
BF16 = jnp.bfloat16


NN = (((1,), (0,)), ((), ()))
NT = (((1,), (1,)), ((), ()))
TN = (((0,), (0,)), ((), ()))
TILES = ((0, 0), (0, 1), (1, 1))


def dot(a, b, form=NN):
    return lax.dot_general(a, b, form, preferred_element_type=F32)


def whole(shape):
    return pl.BlockSpec(shape, lambda *_: (0,) * len(shape))


def cost(flops, nbytes):
    return pl.CostEstimate(flops=int(flops), bytes_accessed=int(nbytes), transcendentals=0)


PARAMS = pltpu.CompilerParams(vmem_limit_bytes=32 * 1024 * 1024)
SCALARS = pl.BlockSpec(memory_space=pltpu.SMEM)


def exchange(value, axis, pairs):
    return lax.ppermute(value, axis, pairs)


def segment_row(seg_ref):
    return seg_ref[0:1, :].astype(F32)


def column_form(row):
    return jnp.transpose(jnp.broadcast_to(row, (WIDTH, row.shape[1])))


def weight_tile(gate, row, column, tile):
    low, high = tile
    times = slice(high * HALF, (high + 1) * HALF)
    sources = slice(low * HALF, (low + 1) * HALF)
    col = column[sources, :]
    same = jnp.concatenate([col, col], axis=1) == row[:, times]
    if low != high:
        weight = jnp.broadcast_to(gate[3:4, times], (HALF, HALF))
        return jnp.where(same, weight, F32(0))
    source = lax.broadcasted_iota(jnp.int32, (HALF, HALF), 0)
    time = lax.broadcasted_iota(jnp.int32, (HALF, HALF), 1)
    differ = jnp.bitwise_xor(source // SPAN, time // SPAN)
    weight = jnp.where(
        differ == 0, gate[0:1, times], jnp.where(differ == 1, gate[1:2, times], gate[2:3, times])
    )
    return jnp.where(same & (source <= time), weight, F32(0))


def summary_kernel(k_ref, v_ref, seg_ref, out_ref):
    row = segment_row(seg_ref)
    last = row[:, ROWS - 1 : ROWS]
    keep = (column_form(row) == last).astype(BF16)
    out_ref[0:MARKS, :] = jnp.broadcast_to(last, (MARKS, WIDTH)).astype(BF16)
    for head in range(HEADS):
        cols = slice(head * WIDTH, (head + 1) * WIDTH)
        state = dot(k_ref[:, cols] * keep, v_ref[:, cols], TN)
        out_ref[MARKS + head * WIDTH : MARKS + (head + 1) * WIDTH, :] = state.astype(BF16)


def summary(k, v, seg):
    return pl.pallas_call(
        summary_kernel,
        out_shape=jax.ShapeDtypeStruct((MARKS + STATE, WIDTH), BF16),
        compiler_params=PARAMS,
        cost_estimate=cost(6.8e7, 1.2e6),
        name="summary",
    )(k, v, seg)


def state_update_kernel(section, index_ref, partner_ref, own_ref, out_ref):
    upper = (index_ref[0] >> section) & 1 == 1
    partner_mark = partner_ref[0:1, :].astype(F32)
    own_mark = own_ref[0:1, :].astype(F32)
    joined = (partner_mark == own_mark).astype(F32)
    partner_scale = jnp.where(upper, joined, F32(1))
    own_scale = jnp.where(upper, F32(1), joined)
    partner = partner_ref[MARKS:, :].astype(F32)
    own = own_ref[MARKS:, :].astype(F32)
    out_ref[MARKS:, :] = (partner * partner_scale + own * own_scale).astype(BF16)
    out_ref[0:MARKS, :] = jnp.where(upper, own_ref[0:MARKS, :], partner_ref[0:MARKS, :])


def state_update(section, index, partner, own):
    return pl.pallas_call(
        functools.partial(state_update_kernel, section),
        out_shape=jax.ShapeDtypeStruct(own.shape, BF16),
        in_specs=[SCALARS, whole(own.shape), whole(own.shape)],
        out_specs=whole(own.shape),
        compiler_params=PARAMS,
        cost_estimate=cost(2e5, 4e5),
        name=f"state_update_{section}",
    )(index, partner, own)


def dual_update_kernel(section, index_ref, partner_ref, own_ref, out_ref):
    upper = (index_ref[0] >> section) & 1 == 1
    partner_mark = partner_ref[0:1, :].astype(F32)
    own_mark = own_ref[0:1, :].astype(F32)
    joined = (partner_mark == own_mark).astype(F32)
    partner_scale = jnp.where(upper, F32(1), joined)
    own_scale = jnp.where(upper, joined, F32(1))
    partner = partner_ref[MARKS + STATE :, :].astype(F32)
    own = own_ref[MARKS + STATE :, :].astype(F32)
    out_ref[MARKS:, :] = (partner * partner_scale + own * own_scale).astype(BF16)
    out_ref[0:MARKS, :] = jnp.where(upper, partner_ref[0:MARKS, :], own_ref[0:MARKS, :])


def dual_update(section, index, partner, own):
    rows = own.shape[0] - STATE
    return pl.pallas_call(
        functools.partial(dual_update_kernel, section),
        out_shape=jax.ShapeDtypeStruct((rows, WIDTH), BF16),
        in_specs=[SCALARS, whole(own.shape), whole(own.shape)],
        out_specs=whole((rows, WIDTH)),
        compiler_params=PARAMS,
        cost_estimate=cost(rows * 512, rows * 768),
        name=f"dual_update_{section}",
    )(index, partner, own)


def near_forward_kernel(q_ref, k_ref, v_ref, gate_ref, seg_ref, out_ref, prob_ref):
    row = segment_row(seg_ref)
    column = column_form(row)
    gate = gate_ref[0]
    out = [None, None]
    for order, (low, high) in enumerate(TILES):
        sources = slice(low * HALF, (low + 1) * HALF)
        times = slice(high * HALF, (high + 1) * HALF)
        scores = dot(k_ref[sources, :], q_ref[times, :], NT)
        probs = (scores * weight_tile(gate, row, column, (low, high))).astype(BF16)
        prob_ref[0, order * HALF : (order + 1) * HALF, :] = probs
        part = dot(v_ref[sources, :], probs, TN)
        out[high] = part if out[high] is None else out[high] + part
    out_ref[0, :, 0:HALF] = out[0]
    out_ref[0, :, HALF:ROWS] = out[1]


def head_columns():
    return pl.BlockSpec((ROWS, WIDTH), lambda h, *_: (0, h))


def head_block(rows, cols):
    return pl.BlockSpec((1, rows, cols), lambda h, *_: (h, 0, 0))


def near_forward(q, k, v, gates, seg):
    return pl.pallas_call(
        near_forward_kernel,
        out_shape=(
            jax.ShapeDtypeStruct((HEADS, WIDTH, ROWS), F32),
            jax.ShapeDtypeStruct((HEADS, 3 * HALF, HALF), BF16),
        ),
        grid=(HEADS,),
        in_specs=[
            head_columns(),
            head_columns(),
            head_columns(),
            head_block(NEAR + FAR, ROWS),
            whole((1, ROWS)),
        ],
        out_specs=(head_block(WIDTH, ROWS), head_block(3 * HALF, HALF)),
        compiler_params=PARAMS,
        cost_estimate=cost(4e8, 4.2e6),
        name="near_forward",
    )(q, k, v, gates, seg)


def far_gates(gate, row, flags=None):
    high_keep = (row == row[:, 0:1]).astype(F32)
    rows = []
    for level in range(FAR):
        scaled = gate[NEAR + level : NEAR + level + 1, :] * high_keep
        rows.append(scaled if flags is None else scaled * flags[level])
    return rows


def piece_flags(index_ref, first, piece_refs):
    flags = []
    for level, piece_ref in enumerate(piece_refs):
        upper = ((index_ref[0] >> level) & 1).astype(F32)
        linked = (piece_ref[0:1, 0:1].astype(F32) == first).astype(F32)
        flags.append(linked * upper)
    return flags


def piece_of(piece_ref, head):
    start = pl.multiple_of(MARKS + head * WIDTH, MARKS)
    return piece_ref[pl.ds(start, WIDTH), :]


def attention_kernel(index_ref, q_ref, near_ref, gate_ref, seg_ref, *rest):
    piece_refs, out_ref = rest[:FAR], rest[FAR]
    head = pl.program_id(0)
    row = segment_row(seg_ref)
    flags = piece_flags(index_ref, row[:, 0:1], piece_refs)
    scales = far_gates(gate_ref[0], row, flags)
    turned = jnp.transpose(q_ref[...].astype(F32))
    scaled = jnp.concatenate([(turned * scale).astype(BF16) for scale in scales], axis=0)
    pieces = jnp.concatenate([piece_of(ref, head) for ref in piece_refs], axis=0)
    out = near_ref[0] + dot(pieces, scaled, TN)
    out_ref[...] = jnp.transpose(out).astype(BF16)


def attention_of(index, q, near, gates, seg, pieces):
    return pl.pallas_call(
        attention_kernel,
        out_shape=jax.ShapeDtypeStruct((ROWS, HEADS * WIDTH), BF16),
        grid=(HEADS,),
        in_specs=[
            SCALARS,
            head_columns(),
            head_block(WIDTH, ROWS),
            head_block(NEAR + FAR, ROWS),
            whole((1, ROWS)),
        ]
        + [whole((MARKS + STATE, WIDTH))] * FAR,
        out_specs=head_columns(),
        compiler_params=PARAMS,
        cost_estimate=cost(3.4e8, 2.8e6),
        name="attention",
    )(index, q, near, gates, seg, *pieces)


def weight_columns(slot):
    return pl.BlockSpec((ROWS, ROWS), lambda i, order, slot=slot: (0, order[slot]))


def grad_partial_kernel(count, order_ref, *refs):
    chunks, weights, out_ref = refs[:count], refs[count : 2 * count], refs[2 * count]
    total = None
    for chunk, weight in zip(chunks, weights):
        part = dot(chunk[...], weight[...], NT)
        total = part if total is None else total + part
    out_ref[...] = total


def grad_partial(order, chunks, slots, weight):
    count = len(chunks)
    tile = pl.BlockSpec((HALF, ROWS), lambda i, order: (i, 0))
    return pl.pallas_call(
        functools.partial(grad_partial_kernel, count),
        out_shape=jax.ShapeDtypeStruct((ROWS, ROWS), F32),
        grid_spec=pltpu.PrefetchScalarGridSpec(
            num_scalar_prefetch=1,
            grid=(2,),
            in_specs=[tile] * count + [weight_columns(slot) for slot in slots],
            out_specs=tile,
        ),
        compiler_params=PARAMS,
        cost_estimate=cost(2.7e8 * count, 1e6 * count + 1e6),
        name="grad_partial",
    )(order, *chunks, *([weight] * count))


def grad_kernel(order_ref, acc_ref, a_ref, b_ref, c0_ref, c1_ref, wa, wb, wc, q_ref, gate_ref, seg_ref, grad_ref, dual_ref):
    row = segment_row(seg_ref)
    high = dot(c0_ref[...], wc[...], NT)
    low = dot(c1_ref[...], wc[...], NT)
    total = acc_ref[...] + dot(a_ref[...], wa[...], NT) + dot(b_ref[...], wb[...], NT)
    total = total + jnp.concatenate([high, low], axis=0)
    grad = total.astype(BF16)
    grad_ref[...] = grad
    dual_ref[0:MARKS, :] = jnp.broadcast_to(row[:, 0:1], (MARKS, WIDTH)).astype(BF16)
    for head in range(HEADS):
        cols = slice(head * WIDTH, (head + 1) * WIDTH)
        turned = jnp.transpose(q_ref[:, cols].astype(F32))
        scales = far_gates(gate_ref[head], row)
        scaled = jnp.concatenate([(turned * scale).astype(BF16) for scale in scales], axis=0)
        leaves = dot(scaled, grad[:, cols]).astype(BF16)
        for level in range(FAR):
            start = MARKS + level * STATE + head * WIDTH
            dual_ref[start : start + WIDTH, :] = leaves[level * WIDTH : (level + 1) * WIDTH, :]


def grad_final(order, acc, chunks, slots, weight, q, gates, seg):
    a, b, c0, c1 = chunks
    rows = MARKS + FAR * STATE
    return pl.pallas_call(
        grad_kernel,
        out_shape=(
            jax.ShapeDtypeStruct((ROWS, ROWS), BF16),
            jax.ShapeDtypeStruct((rows, WIDTH), BF16),
        ),
        grid_spec=pltpu.PrefetchScalarGridSpec(
            num_scalar_prefetch=1,
            grid=(1,),
            in_specs=[whole(x.shape) for x in (acc, a, b, c0, c1)]
            + [weight_columns(slot) for slot in slots]
            + [whole(x.shape) for x in (q, gates, seg)],
            out_specs=(whole((ROWS, ROWS)), whole((rows, WIDTH))),
        ),
        compiler_params=PARAMS,
        cost_estimate=cost(1.2e9, 6e6),
        name="grad_final",
    )(order, acc, a, b, c0, c1, weight, weight, weight, q, gates, seg)


def near_backward_kernel(index_ref, q_ref, k_ref, v_ref, c_ref, prob_ref, gate_ref, seg_ref, *rest):
    piece_refs = rest[:FAR]
    dq_ref, dk_ref, dv_ref = rest[FAR:]
    head = pl.program_id(0)
    row = segment_row(seg_ref)
    column = column_form(row)
    gate = gate_ref[0]
    dq = [None, None]
    dk = [None, None]
    dv = [None, None]

    def add(total, part):
        return part if total is None else total + part

    for order, (low, high) in enumerate(TILES):
        sources = slice(low * HALF, (low + 1) * HALF)
        times = slice(high * HALF, (high + 1) * HALF)
        scores = dot(v_ref[sources, :], c_ref[times, :], NT)
        grads = (scores * weight_tile(gate, row, column, (low, high))).astype(BF16)
        probs = prob_ref[0, order * HALF : (order + 1) * HALF, :]
        dq[high] = add(dq[high], dot(k_ref[sources, :], grads, TN))
        dk[low] = add(dk[low], dot(grads, q_ref[times, :]))
        dv[low] = add(dv[low], dot(probs, c_ref[times, :]))
    flags = piece_flags(index_ref, row[:, 0:1], piece_refs)
    scales = far_gates(gate, row, flags)
    turned = jnp.transpose(c_ref[...].astype(F32))
    scaled = jnp.concatenate([(turned * scale).astype(BF16) for scale in scales], axis=0)
    pieces = jnp.concatenate([piece_of(ref, head) for ref in piece_refs], axis=1)
    total = jnp.concatenate(dq, axis=1) + dot(pieces, scaled)
    dq_ref[...] = jnp.transpose(total).astype(BF16)
    dk_ref[0:HALF, :] = dk[0]
    dk_ref[HALF:ROWS, :] = dk[1]
    dv_ref[0:HALF, :] = dv[0]
    dv_ref[HALF:ROWS, :] = dv[1]


def near_backward(index, q, k, v, grad, probs, gates, seg, pieces):
    return pl.pallas_call(
        near_backward_kernel,
        out_shape=(
            jax.ShapeDtypeStruct((ROWS, ROWS), BF16),
            jax.ShapeDtypeStruct((ROWS, ROWS), F32),
            jax.ShapeDtypeStruct((ROWS, ROWS), F32),
        ),
        grid=(HEADS,),
        in_specs=[SCALARS]
        + [head_columns()] * 4
        + [head_block(3 * HALF, HALF), head_block(NEAR + FAR, ROWS), whole((1, ROWS))]
        + [whole((MARKS + STATE, WIDTH))] * FAR,
        out_specs=(head_columns(),) * 3,
        compiler_params=PARAMS,
        cost_estimate=cost(1.2e9, 7e6),
        name="near_backward",
    )(index, q, k, v, grad, probs, gates, seg, *pieces)


def finish_kernel(index_ref, k_ref, v_ref, dk_ref, dv_ref, seg_ref, *rest):
    dual_refs = rest[:FAR]
    key_ref, value_ref = rest[FAR:]
    head = pl.program_id(0)
    row = segment_row(seg_ref)
    last = row[:, ROWS - 1 : ROWS]
    keep = (column_form(row) == last).astype(F32)
    inbound = None
    for level, dual_ref in enumerate(dual_refs):
        lower = (1 - ((index_ref[0] >> level) & 1)).astype(F32)
        linked = (dual_ref[0:1, 0:1].astype(F32) == last).astype(F32)
        part = piece_of(dual_ref, head).astype(F32) * (linked * lower)
        inbound = part if inbound is None else inbound + part
    inbound = inbound.astype(BF16)
    key_ref[...] = (dk_ref[...] + dot(v_ref[...], inbound, NT) * keep).astype(BF16)
    value_ref[...] = (dv_ref[...] + dot(k_ref[...], inbound) * keep).astype(BF16)


def finish(index, k, v, near_dk, near_dv, seg, duals):
    return pl.pallas_call(
        finish_kernel,
        out_shape=(jax.ShapeDtypeStruct((ROWS, ROWS), BF16),) * 2,
        grid=(HEADS,),
        in_specs=[SCALARS] + [head_columns()] * 4 + [whole((1, ROWS))] + [whole((MARKS + STATE, WIDTH))] * FAR,
        out_specs=(head_columns(),) * 2,
        compiler_params=PARAMS,
        cost_estimate=cost(1.4e8, 4.5e6),
        name="finish",
    )(index, k, v, near_dk, near_dv, seg, *duals)


def mix_first_kernel(order_ref, att_ref, w_ref, right_ref, left_ref):
    part = dot(att_ref[...], w_ref[...])
    right_ref[...] = part[:, 0:HALF].astype(BF16)
    left_ref[...] = part[:, HALF:ROWS].astype(BF16)


def mix_second_kernel(order_ref, att_ref, wr, wl, right_in, left_in, right_ref, left_ref):
    right = dot(att_ref[...], wr[...])
    right_ref[:, 0:HALF] = (right[:, 0:HALF] + right_in[...].astype(F32)).astype(BF16)
    right_ref[:, HALF:ROWS] = right[:, HALF:ROWS].astype(BF16)
    left = dot(att_ref[...], wl[...])
    left_ref[:, HALF:ROWS] = (left[:, HALF:ROWS] + left_in[...].astype(F32)).astype(BF16)
    left_ref[:, 0:HALF] = left[:, 0:HALF].astype(BF16)


def mix_next_kernel(order_ref, att_ref, wr, wl, right_in, left_in, right_ref, left_ref):
    right_ref[...] = (dot(att_ref[...], wr[...]) + right_in[...].astype(F32)).astype(BF16)
    left_ref[...] = (dot(att_ref[...], wl[...]) + left_in[...].astype(F32)).astype(BF16)


def mix_last_kernel(order_ref, att_ref, w_ref, right_in, left_in, out_ref):
    arrived = right_in[...].astype(F32) + left_in[...].astype(F32)
    out_ref[...] = (dot(att_ref[...], w_ref[...]) + arrived).astype(BF16)


def mix(kernel, order, attention, weight, slots, arrived, widths, name):
    def tile(width):
        return pl.BlockSpec((HALF, width), lambda i, order: (i, 0))

    return pl.pallas_call(
        kernel,
        out_shape=tuple(jax.ShapeDtypeStruct((ROWS, width), BF16) for width in widths),
        grid_spec=pltpu.PrefetchScalarGridSpec(
            num_scalar_prefetch=1,
            grid=(2,),
            in_specs=[tile(ROWS)]
            + [weight_columns(slot) for slot in slots]
            + [tile(x.shape[1]) for x in arrived],
            out_specs=tuple(tile(width) for width in widths),
        ),
        compiler_params=PARAMS,
        cost_estimate=cost(2.7e8 * len(slots), 1e6 * len(slots) + 1e6),
        name=name,
    )(order, attention, *([weight] * len(slots)), *arrived)


def shards(queries, keys, values, gates, segment_ids, out_weight, out_grad):
    spread = lax.axis_size("ctx").bit_length() - 1
    groups = lax.axis_size("head")
    index = lax.axis_index("ctx").astype(jnp.int32)[None]
    order = (lax.axis_index("head") + jnp.arange(groups, dtype=jnp.int32)) % groups
    seg = segment_ids.reshape(1, ROWS)
    right = [(source, (source + 1) % groups) for source in range(groups)]
    left = [(source, (source - 1) % groups) for source in range(groups)]

    from_left, from_right = [out_grad], [out_grad]
    for _ in range(3):
        from_left.append(exchange(from_left[-1], "head", right))
        from_right.append(exchange(from_right[-1], "head", left))
    half_a = exchange(from_left[3][:HALF], "head", right)
    half_b = exchange(from_right[3][HALF:], "head", left)

    state = summary(keys, values, seg)
    pieces = []
    for section in range(spread):
        pairs = [(source, source ^ (1 << section)) for source in range(1 << spread)]
        pieces.append(exchange(state, "ctx", pairs))
        if section < spread - 1:
            state = state_update(section, index, pieces[-1], state)
    near_out, probs = near_forward(queries, keys, values, gates, seg)
    attention = attention_of(index, queries, near_out, gates, seg, pieces)

    to_right, to_left = mix(mix_first_kernel, order, attention, out_weight, (4,), (), (HALF, HALF), "mix_0")
    for step, kernel in ((3, mix_second_kernel), (2, mix_next_kernel), (1, mix_next_kernel)):
        arrived = (exchange(to_right, "head", right), exchange(to_left, "head", left))
        to_right, to_left = mix(
            kernel, order, attention, out_weight, (step, groups - step), arrived, (ROWS, ROWS), f"mix_{4 - step}"
        )
    arrived = (exchange(to_right, "head", right), exchange(to_left, "head", left))
    (mixed,) = mix(mix_last_kernel, order, attention, out_weight, (0,), arrived, (ROWS,), "mix_4")

    acc = grad_partial(
        order,
        (out_grad, from_left[1], from_right[1], from_left[2], from_right[2]),
        (0, groups - 1, 1, groups - 2, 2),
        out_weight,
    )
    grad, dual = grad_final(
        order,
        acc,
        (from_left[3], from_right[3], half_a, half_b),
        (groups - 3, 3, 4),
        out_weight,
        queries,
        gates,
        seg,
    )
    duals = []
    for section in range(spread):
        pairs = [(source, source ^ (1 << section)) for source in range(1 << spread)]
        duals.append(exchange(dual, "ctx", pairs))
        if section < spread - 1:
            dual = dual_update(section, index, duals[-1], dual)
    grad_queries, near_dk, near_dv = near_backward(
        index, queries, keys, values, grad, probs, gates, seg, pieces
    )
    grad_keys, grad_values = finish(index, keys, values, near_dk, near_dv, seg, duals)
    return (mixed, grad_queries, grad_keys, grad_values)


def solution(mesh):
    placed = (
        P("ctx", "head"),
        P("ctx", "head"),
        P("ctx", "head"),
        P("head", None, "ctx"),
        P("ctx"),
        P("head", None),
        P("ctx", "head"),
    )
    return jax.shard_map(
        shards,
        mesh=mesh,
        in_specs=placed,
        out_specs=(P("ctx", "head"),) * 4,
        check_vma=False,
    )
```
